256 devices in a mesh: grp: 8 (over x, y_hi), band: 32 (over z, y_lo, core).
Axes of the slice: x: 4, y: 4 (y_hi: 2, y_lo: 2; y = y_hi * 2 + y_lo), z: 8, core: 2. Of those that a mesh axis runs over, the one named last changes fastest.
Arguments:
- orbitals: bfloat16 [128, 64, 4096], P('band'), may hold values from -6 to 6
Outputs:
- exchange: float32 [128, 64, 4096], P('band', 'grp')
The draws below stay inside these ranges and needn't reach their ends.
All inputs are finite; a program needn't handle non-finite values.
Results may differ from the reference program's by a relative error of at most 0.0003.
Values may be sent and summed in bfloat16 or wider, within the bound.
No kernel may reach another device: no remote copies, remote signals or barrier semaphores. Data moves between devices by JAX's collectives and lax.ppermute only.
A program may use at most 128 MiB of HBM per device.

```python
import math
import jax
import jax.numpy as jnp
from jax import lax

GRID = 64
OWN = 4
ROUNDS = 2
BANDS = 128
N_BAND = 32


def level_of(key, shape, split, low, largest):
    def one(axis_at, shards_of):
        draws = jax.random.uniform(jax.random.fold_in(jax.random.fold_in(key, 6), axis_at), (shards_of,), jnp.float32, low / len(split), largest / len(split))
        return jnp.repeat(jnp.exp(draws), shape[axis_at] // shards_of).reshape((-1,) + (1,) * (len(shape) - axis_at - 1))

    loudness = one(*split[0])
    for cut in split[1:]:
        loudness = loudness * one(*cut)
    return loudness


def scatter_about(own_key, dims, scale, bound, shards=(), held_as=jnp.bfloat16):
    drawn = jax.random.normal(own_key, dims, jnp.float32) * scale
    if len(shards) > 0:
        drawn = level_of(own_key, dims, shards, -0.22, 0.18) * drawn
    return jnp.clip(drawn, min=-bound, max=bound).astype(held_as)


def setup_inputs(seed: int = 0) -> dict:
    key_of = jax.random.split(jax.random.key(seed), 2)
    return {
        "orbitals": scatter_about(key_of[0], (BANDS, GRID, GRID * GRID), 1.0, 6.0, ((0, 32),)),
    }


CELL_LENGTH = 41.05
SCREENING = 0.106


def kernel_table(grid):
    wavenum = jnp.arange(grid, dtype=jnp.int32)
    wavenum = jnp.where(wavenum < grid // 2, wavenum, wavenum - grid).astype(jnp.float32) * (2.0 * math.pi / CELL_LENGTH)
    squared = wavenum[:, None, None] ** 2 + wavenum[None, :, None] ** 2 + wavenum[None, None, :] ** 2
    safe = jnp.where(squared > 0, squared, 1.0)
    screened = 4.0 * math.pi * (1.0 - jnp.exp(-safe / (4.0 * SCREENING * SCREENING))) / safe
    return jnp.where(squared > 0, screened, math.pi / (SCREENING * SCREENING)).astype(jnp.float32)


def reference(orbitals):
    fields = orbitals.astype(jnp.float32).reshape(BANDS, GRID, GRID, GRID)
    kernel = kernel_table(GRID)
    distances = jnp.array([d for r in range(1, ROUNDS + 1) for d in (r, -r)], dtype=jnp.int32)
    members = jnp.arange(OWN, dtype=jnp.int32)

    def exchange_band(band_index):
        block = band_index // OWN
        partners = (((block + distances[:, None]) % N_BAND) * OWN + members[None, :]).reshape(-1)
        partner_fields = fields[partners]
        density = fields[band_index][None] * partner_fields
        spectrum = jnp.fft.fftn(density, axes=(1, 2, 3)) * kernel
        potential = jnp.real(jnp.fft.ifftn(spectrum, axes=(1, 2, 3)))
        return -0.25 * jnp.sum(partner_fields * potential, axis=0)

    result = lax.map(exchange_band, jnp.arange(BANDS, dtype=jnp.int32))
    return result.reshape(BANDS, GRID, GRID * GRID)
```

```python
import functools
import math

import jax
import jax.numpy as jnp
import ml_dtypes
import numpy as np
from jax import lax
from jax.experimental import pallas as pl
from jax.experimental.pallas import tpu as pltpu
from jax.sharding import PartitionSpec as P

CELL_LENGTH = 41.05
SCREENING = 0.106
G = 64
T = 256

def split_np(m):
    hi = m.astype(ml_dtypes.bfloat16)
    lo = (m - hi.astype(np.float64)).astype(ml_dtypes.bfloat16)
    return hi, lo

def tables():
    i = np.arange(G)
    ang = 2 * np.pi * ((i[:, None] * i[None, :]) % G) / G
    h = (np.cos(ang) + np.sin(ang)) / 8.0
    r = np.arange(T)
    z_in = (r[:, None] % 4 == r[None, :] // G) * h[r[:, None] // 4, r[None, :] % G]
    y = 4 * (r // 16) + r % 4
    y_both = ((r[:, None] // 4 % 4) == (r[None, :] // 4 % 4)) * h[y[:, None], y[None, :]]
    x_both = np.kron(np.eye(4), h)
    out = []
    for m in (z_in, z_in.T, y_both, x_both):
        out += list(split_np(m))
    return [jnp.asarray(o) for o in out]

def kernel_table():
    s = (T // 16, T, 128)
    j = lax.broadcasted_iota(jnp.int32, s, 0)
    r = lax.broadcasted_iota(jnp.int32, s, 1)
    l = lax.broadcasted_iota(jnp.int32, s, 2)
    def w(k):
        return jnp.where(k < G // 2, k, k - G)
    a, b, c = w(l % G), w(4 * (r // 16) + r % 4), w(4 * j + r // 4 % 4)
    q = (a * a + b * b + c * c).astype(jnp.float32)
    squared = q * (2.0 * math.pi / CELL_LENGTH) ** 2
    safe = jnp.where(squared > 0, squared, 1.0)
    screened = 4.0 * math.pi * (1.0 - jnp.exp(-safe / (4.0 * SCREENING * SCREENING))) / safe
    return -0.25 * jnp.where(squared > 0, screened, math.pi / (SCREENING * SCREENING))

NN = (((1,), (0,)), ((), ()))
NT = (((1,), (1,)), ((), ()))
def dot(a, b, dims):
    return lax.dot_general(a, b, dims, preferred_element_type=jnp.float32)

def split(v):
    hi = v.astype(jnp.bfloat16)
    return hi, (v - hi.astype(jnp.float32)).astype(jnp.bfloat16)

def dot3(a, b, dims):
    return dot(a[0], b[0], dims) + (dot(a[0], b[1], dims) + dot(a[1], b[0], dims))

def pair_kernel(unroll, first, *refs):
    if first:
        own, pa, pb, zih, zil, zoh, zol, yh, yl, xh, xl, kt, out, bh, bl = refs
    else:
        own, pa, pb, acc, zih, zil, zoh, zol, yh, yl, xh, xl, kt, out, bh, bl = refs
    n = T // 16

    def lanes(t):
        return pl.ds(pl.multiple_of(t * T, T), T)

    def partners(t):
        return jnp.concatenate([pa[:, :, lanes(t)], pb[:, :, lanes(t)]], axis=0)

    def step_in(t, c):
        phi = own[:, lanes(t)].astype(jnp.float32)
        d = partners(t).astype(jnp.float32) * phi[None]
        v = dot3((zih[...], zil[...]), split(d.reshape(T, T)), NT)
        bh[t], bl[t] = split(v)
        return c

    def step_mid(j, c):
        rows = pl.ds(pl.multiple_of(j * 16, 16), 16)
        d = (bh[:, rows, :].reshape(T, T), bl[:, rows, :].reshape(T, T))
        y, x = (yh[...], yl[...]), (xh[...], xl[...])
        v = dot3(d, x, NN)
        v = dot3(y, split(v), NN)
        k = kt[j]
        v = v * jnp.concatenate([k, k], axis=1)
        v = dot3(y, split(v), NN)
        v = dot3(split(v), x, NN)
        hi, lo = split(v)
        bh[:, rows, :] = hi.reshape(n, 16, T)
        bl[:, rows, :] = lo.reshape(n, 16, T)
        return c

    row = lax.broadcasted_iota(jnp.int32, (T, T), 0)
    col = lax.broadcasted_iota(jnp.int32, (T, T), 1)
    eye = (row == col).astype(jnp.float32).astype(jnp.bfloat16)
    fold = (row[:G] == col[:G] % G).astype(jnp.float32).astype(jnp.bfloat16)

    def step_out(t, c):
        v = dot3((zoh[...], zol[...]), (bh[t], bl[t]), NN)
        phi = dot(eye, partners(t).reshape(T, T), NT)
        hi, lo = split(v * phi)
        v = dot(fold, hi, NT) + dot(fold, lo, NT)
        out[:, lanes(t)] = v if first else acc[:, lanes(t)] + v
        return c

    lax.fori_loop(0, n, step_in, 0, unroll=unroll)
    lax.fori_loop(0, n, step_mid, 0, unroll=unroll)
    lax.fori_loop(0, n, step_out, 0, unroll=unroll)


def pair_terms(own, pa, pb, acc, tabs, kt, unroll=4):
    vm = pl.BlockSpec(memory_space=pltpu.VMEM)
    first = acc is None
    args = (own, pa, pb) + (() if first else (acc,)) + (*tabs, kt)
    return pl.pallas_call(
        functools.partial(pair_kernel, unroll, first),
        out_shape=jax.ShapeDtypeStruct((G, G * G), jnp.float32),
        in_specs=[vm] * len(args),
        out_specs=vm,
        scratch_shapes=[pltpu.VMEM((T // 16, T, T), jnp.bfloat16)] * 2,
        compiler_params=pltpu.CompilerParams(vmem_limit_bytes=40 * 1024 * 1024),
        cost_estimate=pl.CostEstimate(flops=20 * 16 * 2 * T**3, bytes_accessed=8 << 20, transcendentals=0),
        name="pair_first" if first else "pair_second",
    )(*args)


def body(orbitals):
    groups, blocks = lax.axis_size("grp"), lax.axis_size("band")
    far = groups // 2

    def source(g, b, distance):
        s = (b + distance) % blocks
        crosses = b // 4 != s // 4
        return (g ^ 1 if crosses else g) * blocks + s

    def moves(near_of, far_of):
        pairs = []
        for g in range(groups):
            for b in range(blocks):
                d = (near_of if g < far else far_of)[b % 2]
                pairs.append((source(g, b, d), g * blocks + b))
        return pairs

    def move(v, near_of, far_of):
        return lax.ppermute(v, ("grp", "band"), moves(near_of, far_of))

    is_far = lax.axis_index("grp") >= far
    swap = (1, -1)
    low, high = orbitals[:2], orbitals[2:]
    part_a = move(low, swap, (-1, 1))
    part_b = move(jnp.where(is_far, part_a, high), swap, swap)
    part_a, later_c, later_d = lax.optimization_barrier((part_a, jnp.where(is_far, high, low), high))
    part_c = move(later_c, (-2, 2), (-1, 1))
    part_d = move(later_d, (-2, 2), (2, -2))
    own = lax.dynamic_index_in_dim(orbitals, lax.axis_index("grp") % far, 0, keepdims=False)
    tabs, kt = tables(), kernel_table()
    row = pair_terms(own, part_a, part_b, None, tabs, kt)
    row = pair_terms(own, part_c, part_d, row, tabs, kt)
    slabs = row.reshape(groups, G // groups, G * G)
    slabs = lax.all_to_all(slabs, "grp", split_axis=0, concat_axis=0, tiled=True)
    return slabs[:far] + slabs[far:]


def solution(mesh):
    return jax.shard_map(
        body,
        mesh=mesh,
        in_specs=(P("band", None, None),),
        out_specs=P("band", "grp", None),
        check_vma=False,
    )
```

```python
import functools
import math

import jax
import jax.numpy as jnp
import ml_dtypes
import numpy as np
from jax import lax
from jax.experimental import pallas as pl
from jax.experimental.pallas import tpu as pltpu
from jax.sharding import PartitionSpec as P

CELL_LENGTH = 41.05
SCREENING = 0.106
G = 64
H = 128
T = 256


def split_table(m):
    hi = m.astype(ml_dtypes.bfloat16)
    lo = (m - hi.astype(np.float64)).astype(ml_dtypes.bfloat16)
    return np.block([[hi, hi], [lo, lo]])


def row_of(kind, r):
    s, kz, y = r % 8 // 4, r // 2 % 2, r % 2
    return 4 * (r // 8) + 2 * (s ^ kind) + y, 2 * kind + kz


def tables():
    i = np.arange(G)
    ang = 2 * np.pi * ((i[:, None] * i[None, :]) % G) / G
    h = (np.cos(ang) + np.sin(ang)) / 8.0
    r = np.arange(H)
    out = []
    for kind in range(2):
        kz = 4 * (r // 8) + 2 * ((r // 4 % 2) ^ kind) + r // 2 % 2
        m = (r[:, None] % 2 == r[None, :] // G) * h[kz[:, None], r[None, :] % G]
        out += [split_table(m), split_table(m.T)]
    for kind in range(2):
        y, kz = row_of(kind, r)
        out.append(split_table((kz[:, None] == kz[None, :]) * h[y[:, None], y[None, :]]))
    out.append(split_table(np.kron(np.eye(2), h)).T)
    return [jnp.asarray(o) for o in out]


def kernel_table():
    s = (T // 8, H, H)
    j = lax.broadcasted_iota(jnp.int32, s, 0)
    r = lax.broadcasted_iota(jnp.int32, s, 1)
    l = lax.broadcasted_iota(jnp.int32, s, 2)

    def wave(k):
        return jnp.where(k < G // 2, k, k - G)

    y, kz = row_of(j % 2, r)
    a, b, c = wave(l % G), wave(y), wave(4 * (j // 2) + kz)
    q = (a * a + b * b + c * c).astype(jnp.float32)
    squared = q * (2.0 * math.pi / CELL_LENGTH) ** 2
    safe = jnp.where(squared > 0, squared, 1.0)
    screened = 4.0 * math.pi * (1.0 - jnp.exp(-safe / (4.0 * SCREENING * SCREENING))) / safe
    return -0.25 * jnp.where(squared > 0, screened, math.pi / (SCREENING * SCREENING))


NN = (((1,), (0,)), ((), ()))
NT = (((1,), (1,)), ((), ()))


def dot(a, b, dims):
    return lax.dot_general(a, b, dims, preferred_element_type=jnp.float32)


def split(v, axis):
    hi = v.astype(jnp.bfloat16)
    lo = (v - hi.astype(jnp.float32)).astype(jnp.bfloat16)
    return jnp.concatenate([hi, lo], axis=axis)


def pair_kernel(unroll, first, *refs):
    ui, um, uo = unroll
    if first:
        own, pa, pb, zia, zoa, zib, zob, y0, y1, xw, kt, out, buf = refs
    else:
        own, pa, pb, acc, zia, zoa, zib, zob, y0, y1, xw, kt, out, buf = refs
    n = T // 16
    low = lax.broadcasted_iota(jnp.int32, (n, 8, T), 1) < 4

    def lanes(t, size=T):
        return pl.ds(pl.multiple_of(t * size, size), size)

    def partners(t, size=T):
        return jnp.concatenate([pa[:, :, lanes(t, size)], pb[:, :, lanes(t, size)]], axis=0)

    def step_in(i, c):
        ts = [i * ui + k for k in range(ui)]

        def product(u):
            phi = own[:, lanes(u, H)].astype(jnp.float32)
            return split((partners(u, H).astype(jnp.float32) * phi[None]).reshape(T, H), 1)

        ds = [(product(2 * t + s), (zia, zib)[s]) for t in ts for s in range(2)]
        vs = [dot(w[...], d, NT) for d, w in ds]
        vs = [(v[:H] + v[H:]).reshape(n, 8, T) for v in vs]
        for k, t in enumerate(ts):
            a, b = vs[2 * k], vs[2 * k + 1]
            buf[t] = jnp.stack([jnp.where(low, a, b), jnp.where(low, b, a)], axis=1).reshape(T, T)
        return c

    def along_x(vs):
        vs = [jnp.concatenate([split(v[:, :H], 1), split(v[:, H:], 1)], axis=0) for v in vs]
        vs = [dot(v, xw[...], NN) for v in vs]
        vs = [v[:, :H] + v[:, H:] for v in vs]
        return [jnp.concatenate([v[:H], v[H:]], axis=1) for v in vs]

    def along_y(vs, ws):
        vs = [split(v, 0) for v in vs]
        vs = [dot(w[...], v, NN) for v, w in zip(vs, ws)]
        return [v[:H] + v[H:] for v in vs]

    def step_mid(i, c):
        js = [i * um + k for k in range(um)]
        at = [(j, kind) for j in js for kind in range(2)]
        rows = [pl.ds(pl.multiple_of(j * 16 + 8 * kind, 8), 8) for j, kind in at]
        ws = [(y0, y1)[kind] for _, kind in at]
        vs = [buf[:, r, :].reshape(H, T) for r in rows]
        vs = along_y(along_x(vs), ws)
        ks = [kt[2 * j + kind] for j, kind in at]
        vs = [v * jnp.concatenate([k, k], axis=1) for v, k in zip(vs, ks)]
        vs = along_x(along_y(vs, ws))
        for r, v in zip(rows, vs):
            buf[:, r, :] = v.reshape(n, 8, T)
        return c

    row = lax.broadcasted_iota(jnp.int32, (T, T), 0)
    col = lax.broadcasted_iota(jnp.int32, (T, T), 1)
    eye = (row == col).astype(jnp.float32).astype(jnp.bfloat16)
    fold = (row[:G] == col[:G] % G).astype(jnp.float32).astype(jnp.bfloat16)

    def step_out(i, c):
        ts = [i * uo + k for k in range(uo)]
        phis = [dot(eye, partners(t).reshape(T, T), NT) for t in ts]
        vs = []
        for t in ts:
            v = buf[t].reshape(n, 2, 8, T)
            vs.append((jnp.where(low, v[:, 0], v[:, 1]), zoa))
            vs.append((jnp.where(low, v[:, 1], v[:, 0]), zob))
        vs = [(split(v.reshape(H, T), 0), w) for v, w in vs]
        vs = [dot(w[...], v, NN) for v, w in vs]
        vs = [v[:H] + v[H:] for v in vs]
        vs = [v * phis[k // 2][H * (k % 2) : H * (k % 2) + H] for k, v in enumerate(vs)]
        vs = [split(v[:, :H] + v[:, H:], 1) for v in vs]
        for k, t in enumerate(ts):
            v = dot(fold, jnp.concatenate(vs[2 * k : 2 * k + 2], axis=0), NT)
            out[:, lanes(t)] = v if first else acc[:, lanes(t)] + v
        return c

    lax.fori_loop(0, n // ui, step_in, 0)
    lax.fori_loop(0, n // um, step_mid, 0)
    lax.fori_loop(0, n // uo, step_out, 0)


def pair_terms(own, pa, pb, acc, tabs, kt, unroll=(4, 4, 4)):
    vm = pl.BlockSpec(memory_space=pltpu.VMEM)
    first = acc is None
    args = (own, pa, pb) + (() if first else (acc,)) + (*tabs, kt)
    return pl.pallas_call(
        functools.partial(pair_kernel, unroll, first),
        out_shape=jax.ShapeDtypeStruct((G, G * G), jnp.float32),
        in_specs=[vm] * len(args),
        out_specs=vm,
        scratch_shapes=[pltpu.VMEM((T // 16, T, T), jnp.float32)],
        compiler_params=pltpu.CompilerParams(vmem_limit_bytes=40 * 1024 * 1024),
        cost_estimate=pl.CostEstimate(flops=13 * 16 * 2 * T**3, bytes_accessed=8 << 20, transcendentals=0),
        name="pair_first" if first else "pair_second",
    )(*args)


def body(orbitals):
    groups, blocks = lax.axis_size("grp"), lax.axis_size("band")
    far = groups // 2

    def source(g, b, distance):
        s = (b + distance) % blocks
        crosses = b // 4 != s // 4
        return (g ^ 1 if crosses else g) * blocks + s

    def moves(near_of, far_of):
        pairs = []
        for g in range(groups):
            for b in range(blocks):
                d = (near_of if g < far else far_of)[b % 2]
                pairs.append((source(g, b, d), g * blocks + b))
        return pairs

    def move(v, near_of, far_of):
        return lax.ppermute(v, ("grp", "band"), moves(near_of, far_of))

    is_far = lax.axis_index("grp") >= far
    swap = (1, -1)
    low, high = orbitals[:2], orbitals[2:]
    part_a = move(low, swap, (-1, 1))
    part_b = move(jnp.where(is_far, part_a, high), swap, swap)
    part_a, later_c, later_d = lax.optimization_barrier((part_a, jnp.where(is_far, high, low), high))
    part_c = move(later_c, (-2, 2), (-1, 1))
    part_d = move(later_d, (-2, 2), (2, -2))
    own = lax.dynamic_index_in_dim(orbitals, lax.axis_index("grp") % far, 0, keepdims=False)
    tabs, kt = tables(), kernel_table()
    row = pair_terms(own, part_a, part_b, None, tabs, kt)
    row = pair_terms(own, part_c, part_d, row, tabs, kt)
    slabs = row.reshape(groups, G // groups, G * G)
    slabs = lax.all_to_all(slabs, "grp", split_axis=0, concat_axis=0, tiled=True)
    return slabs[:far] + slabs[far:]


def solution(mesh):
    return jax.shard_map(
        body,
        mesh=mesh,
        in_specs=(P("band", None, None),),
        out_specs=P("band", "grp", None),
        check_vma=False,
    )
```

```python
import functools
import math

import jax
import jax.numpy as jnp
import ml_dtypes
import numpy as np
from jax import lax
from jax.experimental import pallas as pl
from jax.experimental.pallas import tpu as pltpu
from jax.sharding import PartitionSpec as P

CELL_LENGTH = 41.05
SCREENING = 0.106
G = 64
H = 128
T = 256


def split_table(m):
    hi = m.astype(ml_dtypes.bfloat16)
    lo = (m - hi.astype(np.float64)).astype(ml_dtypes.bfloat16)
    return np.block([[hi, hi], [lo, lo]])


def row_of(kind, r):
    s, kz, y = r % 8 // 4, r // 2 % 2, r % 2
    return 4 * (r // 8) + 2 * (s ^ kind) + y, 2 * kind + kz


def tables():
    i = np.arange(G)
    ang = 2 * np.pi * ((i[:, None] * i[None, :]) % G) / G
    h = (np.cos(ang) + np.sin(ang)) / 8.0
    r = np.arange(H)
    out = []
    for kind in range(2):
        kz = 4 * (r // 8) + 2 * ((r // 4 % 2) ^ kind) + r // 2 % 2
        m = (r[:, None] % 2 == r[None, :] // G) * h[kz[:, None], r[None, :] % G]
        out += [split_table(m), split_table(m.T)]
    for kind in range(2):
        y, kz = row_of(kind, r)
        out.append(split_table((kz[:, None] == kz[None, :]) * h[y[:, None], y[None, :]]))
    out.append(split_table(np.kron(np.eye(2), h)).T)
    return jnp.asarray(np.stack(out))


def kernel_table():
    s = (T // 8, H, H)
    j = lax.broadcasted_iota(jnp.int32, s, 0)
    r = lax.broadcasted_iota(jnp.int32, s, 1)
    l = lax.broadcasted_iota(jnp.int32, s, 2)

    def wave(k):
        return jnp.where(k < G // 2, k, k - G)

    y, kz = row_of(j % 2, r)
    a, b, c = wave(l % G), wave(y), wave(4 * (j // 2) + kz)
    q = (a * a + b * b + c * c).astype(jnp.float32)
    squared = q * (2.0 * math.pi / CELL_LENGTH) ** 2
    safe = jnp.where(squared > 0, squared, 1.0)
    screened = 4.0 * math.pi * (1.0 - jnp.exp(-safe / (4.0 * SCREENING * SCREENING))) / safe
    return -0.25 * jnp.where(squared > 0, screened, math.pi / (SCREENING * SCREENING))


NN = (((1,), (0,)), ((), ()))
NT = (((1,), (1,)), ((), ()))


def dot(a, b, dims):
    return lax.dot_general(a, b, dims, preferred_element_type=jnp.float32)


def split(v, axis):
    hi = v.astype(jnp.bfloat16)
    lo = (v - hi.astype(jnp.float32)).astype(jnp.bfloat16)
    return jnp.concatenate([hi, lo], axis=axis)


def pair_kernel(steps, first, *refs):
    ui, um, uo = steps
    own, pa, pb, pc, tabs, kt = refs[:6]
    acc = None if first else refs[6]
    out, buf = refs[-2:]
    zia, zoa, zib, zob, y0, y1, xw = (tabs.at[k] for k in range(7))
    n = T // 16
    low = lax.broadcasted_iota(jnp.int32, (n, 8, T), 1) < 4

    def lanes(t, size=T):
        return pl.ds(pl.multiple_of(t * size, size), size)

    def partners(t, size=T):
        return jnp.concatenate([p[:, :, lanes(t, size)] for p in (pa, pb, pc)], axis=0)

    def step_in(i, c):
        ts = [i * ui + k for k in range(ui)]

        def product(u):
            phi = own[:, :, lanes(u, H)].astype(jnp.float32)
            return split((partners(u, H).astype(jnp.float32) * phi).reshape(T, H), 1)

        ds = [(product(2 * t + s), (zia, zib)[s]) for t in ts for s in range(2)]
        vs = [dot(w[...], d, NT) for d, w in ds]
        vs = [(v[:H] + v[H:]).reshape(n, 8, T) for v in vs]
        for k, t in enumerate(ts):
            a, b = vs[2 * k], vs[2 * k + 1]
            buf[t] = jnp.stack([jnp.where(low, a, b), jnp.where(low, b, a)], axis=1).reshape(T, T)
        return c

    def along_x(vs):
        vs = [jnp.concatenate([split(v[:, :H], 1), split(v[:, H:], 1)], axis=0) for v in vs]
        vs = [dot(v, xw[...], NN) for v in vs]
        vs = [v[:, :H] + v[:, H:] for v in vs]
        return [jnp.concatenate([v[:H], v[H:]], axis=1) for v in vs]

    def along_y(vs, ws):
        vs = [split(v, 0) for v in vs]
        vs = [dot(w[...], v, NN) for v, w in zip(vs, ws)]
        return [v[:H] + v[H:] for v in vs]

    def step_mid(i, c):
        js = [i * um + k for k in range(um)]
        at = [(j, kind) for j in js for kind in range(2)]
        rows = [pl.ds(pl.multiple_of(j * 16 + 8 * kind, 8), 8) for j, kind in at]
        ws = [(y0, y1)[kind] for _, kind in at]
        vs = [buf[:, r, :].reshape(H, T) for r in rows]
        vs = along_y(along_x(vs), ws)
        ks = [kt[2 * j + kind] for j, kind in at]
        vs = [v * jnp.concatenate([k, k], axis=1) for v, k in zip(vs, ks)]
        vs = along_x(along_y(vs, ws))
        for r, v in zip(rows, vs):
            buf[:, r, :] = v.reshape(n, 8, T)
        return c

    row = lax.broadcasted_iota(jnp.int32, (T, T), 0)
    col = lax.broadcasted_iota(jnp.int32, (T, T), 1)
    eye = (row == col).astype(jnp.float32).astype(jnp.bfloat16)
    fold = (row[:G] == col[:G] % G).astype(jnp.float32).astype(jnp.bfloat16)

    def step_out(i, c):
        ts = [i * uo + k for k in range(uo)]
        phis = [dot(eye, partners(t).reshape(T, T), NT) for t in ts]
        vs = []
        for t in ts:
            v = buf[t].reshape(n, 2, 8, T)
            vs.append((jnp.where(low, v[:, 0], v[:, 1]), zoa))
            vs.append((jnp.where(low, v[:, 1], v[:, 0]), zob))
        vs = [(split(v.reshape(H, T), 0), w) for v, w in vs]
        vs = [dot(w[...], v, NN) for v, w in vs]
        vs = [v[:H] + v[H:] for v in vs]
        vs = [v * phis[k // 2][H * (k % 2) : H * (k % 2) + H] for k, v in enumerate(vs)]
        vs = [split(v[:, :H] + v[:, H:], 1) for v in vs]
        for k, t in enumerate(ts):
            v = dot(fold, jnp.concatenate(vs[2 * k : 2 * k + 2], axis=0), NT)
            out[:, lanes(t)] = v if first else acc[:, lanes(t)] + v
        return c

    lax.fori_loop(0, n // ui, step_in, 0)
    lax.fori_loop(0, n // um, step_mid, 0)
    lax.fori_loop(0, n // uo, step_out, 0)


def pair_terms(own, parts, acc, tabs, kt, steps=(8, 8, 8)):
    vm = pl.BlockSpec(memory_space=pltpu.VMEM)
    first = acc is None
    args = (own, *parts, tabs, kt) + (() if first else (acc,))
    return pl.pallas_call(
        functools.partial(pair_kernel, steps, first),
        out_shape=jax.ShapeDtypeStruct((G, G * G), jnp.float32),
        in_specs=[vm] * len(args),
        out_specs=vm,
        scratch_shapes=[pltpu.VMEM((T // 16, T, T), jnp.float32)],
        compiler_params=pltpu.CompilerParams(vmem_limit_bytes=40 * 1024 * 1024),
        cost_estimate=pl.CostEstimate(flops=13 * 16 * 2 * T**3, bytes_accessed=8 << 20, transcendentals=0),
        name="pair_first" if first else "pair_second",
    )(*args)


def pick_kernel(at, orbitals, low, high, both, own, sems):
    half = 2 * at[0]
    copies = [
        pltpu.make_async_copy(orbitals.at[pl.ds(half, 1)], low, sems.at[0]),
        pltpu.make_async_copy(orbitals.at[pl.ds(half + 1, 1)], high, sems.at[1]),
        pltpu.make_async_copy(orbitals.at[pl.ds(half, 2)], both, sems.at[2]),
        pltpu.make_async_copy(orbitals.at[pl.ds(at[1], 1)], own, sems.at[3]),
    ]
    for copy in copies:
        copy.start()
    for copy in copies:
        copy.wait()


def pick(orbitals, half, mine):
    vm = pl.BlockSpec(memory_space=pltpu.VMEM)
    return pl.pallas_call(
        pick_kernel,
        out_shape=[jax.ShapeDtypeStruct((k, *orbitals.shape[1:]), orbitals.dtype) for k in (1, 1, 2, 1)],
        in_specs=[pl.BlockSpec(memory_space=pltpu.SMEM), pl.BlockSpec(memory_space=pl.ANY)],
        out_specs=[vm] * 4,
        scratch_shapes=[pltpu.SemaphoreType.DMA((4,))],
        compiler_params=pltpu.CompilerParams(vmem_limit_bytes=8 * 1024 * 1024),
        name="pick",
    )(jnp.stack([half, mine]).astype(jnp.int32), orbitals)


def body(orbitals):
    groups, blocks = lax.axis_size("grp"), lax.axis_size("band")
    halves = groups // 2

    def source(g, b, distance):
        s = (b + distance) % blocks
        crosses = b // 4 != s // 4
        return (g ^ 1 if crosses else g) * blocks + s

    def move(v, distances):
        pairs = [(source(g, b, distances[b % 2]), g * blocks + b) for g in range(groups) for b in range(blocks)]
        return lax.ppermute(v, ("grp", "band"), pairs)

    chip, near, far = (1, -1), (-1, 1), (-2, 2)
    group = lax.axis_index("grp")
    low, high, both, own = pick(orbitals, group // halves, group % halves)
    near_low = move(low, near)
    on_chip = move(both, chip)
    near_high = move(high, near)
    near_low, both, kt = lax.optimization_barrier((near_low, both, kernel_table()))
    far_both = move(both, far)
    swapped_low = move(near_low, chip)
    tabs = tables()
    row = pair_terms(own, (on_chip, near_low, swapped_low), None, tabs, kt)
    swapped_high = move(near_high, chip)
    row = pair_terms(own, (far_both, near_high, swapped_high), row, tabs, kt)
    slabs = row.reshape(groups, G // groups, G * G)
    slabs = lax.all_to_all(slabs, "grp", split_axis=0, concat_axis=0, tiled=True)
    return slabs[:halves] + slabs[halves:]


def solution(mesh):
    return jax.shard_map(
        body,
        mesh=mesh,
        in_specs=(P("band", None, None),),
        out_specs=P("band", "grp", None),
        check_vma=False,
    )
```

```python
import functools
import math

import jax
import jax.numpy as jnp
import ml_dtypes
import numpy as np
from jax import lax
from jax.experimental import pallas as pl
from jax.experimental.pallas import tpu as pltpu
from jax.sharding import PartitionSpec as P

CELL_LENGTH = 41.05
SCREENING = 0.106
G = 64
H = 128
T = 256


def split_table(m):
    hi = m.astype(ml_dtypes.bfloat16)
    lo = (m - hi.astype(np.float64)).astype(ml_dtypes.bfloat16)
    return np.block([[hi, hi], [lo, lo]])


def row_of(kind, r):
    s, kz, y = r % 8 // 4, r // 2 % 2, r % 2
    return 4 * (r // 8) + 2 * (s ^ kind) + y, 2 * kind + kz


def tables():
    i = np.arange(G)
    ang = 2 * np.pi * ((i[:, None] * i[None, :]) % G) / G
    h = (np.cos(ang) + np.sin(ang)) / 8.0
    r = np.arange(H)
    out = []
    for kind in range(2):
        kz = 4 * (r // 8) + 2 * ((r // 4 % 2) ^ kind) + r // 2 % 2
        m = (r[:, None] % 2 == r[None, :] // G) * h[kz[:, None], r[None, :] % G]
        out += [split_table(m), split_table(m.T)]
    for kind in range(2):
        y, kz = row_of(kind, r)
        out.append(split_table((kz[:, None] == kz[None, :]) * h[y[:, None], y[None, :]]))
    out.append(split_table(np.kron(np.eye(2), h)).T)
    return jnp.asarray(np.stack(out))


def kernel_table():
    s = (T // 8, H, H)
    j = lax.broadcasted_iota(jnp.int32, s, 0)
    r = lax.broadcasted_iota(jnp.int32, s, 1)
    l = lax.broadcasted_iota(jnp.int32, s, 2)

    def wave(k):
        return jnp.where(k < G // 2, k, k - G)

    y, kz = row_of(j % 2, r)
    a, b, c = wave(l % G), wave(y), wave(4 * (j // 2) + kz)
    q = (a * a + b * b + c * c).astype(jnp.float32)
    squared = q * (2.0 * math.pi / CELL_LENGTH) ** 2
    safe = jnp.where(squared > 0, squared, 1.0)
    screened = 4.0 * math.pi * (1.0 - jnp.exp(-safe / (4.0 * SCREENING * SCREENING))) / safe
    return -0.25 * jnp.where(squared > 0, screened, math.pi / (SCREENING * SCREENING))


NN = (((1,), (0,)), ((), ()))
NT = (((1,), (1,)), ((), ()))


def dot(a, b, dims):
    return lax.dot_general(a, b, dims, preferred_element_type=jnp.float32)


def split(v, axis):
    hi = v.astype(jnp.bfloat16)
    lo = (v - hi.astype(jnp.float32)).astype(jnp.bfloat16)
    return jnp.concatenate([hi, lo], axis=axis)


def pair_kernel(steps, first, *refs):
    ui, um, uo = steps
    own, pa, pb, pc, tabs, kt = refs[:6]
    acc = None if first else refs[6]
    out, buf = refs[-2:]
    zia, zoa, zib, zob, y0, y1, xw = (tabs.at[k] for k in range(7))
    n = T // 16
    low = lax.broadcasted_iota(jnp.int32, (n, 8, T), 1) < 4

    def lanes(t, size=T):
        return pl.ds(pl.multiple_of(t * size, size), size)

    def partners(t, size=T):
        return jnp.concatenate([p[:, :, lanes(t, size)] for p in (pa, pb, pc)], axis=0)

    def step_in(i, c):
        ts = [i * ui + k for k in range(ui)]

        def product(u):
            phi = own[:, :, lanes(u, H)].astype(jnp.float32)
            return split((partners(u, H).astype(jnp.float32) * phi).reshape(T, H), 1)

        ds = [(product(2 * t + s), (zia, zib)[s]) for t in ts for s in range(2)]
        vs = [dot(w[...], d, NT) for d, w in ds]
        vs = [(v[:H] + v[H:]).reshape(n, 8, T) for v in vs]
        for k, t in enumerate(ts):
            a, b = vs[2 * k], vs[2 * k + 1]
            buf[t] = jnp.stack([jnp.where(low, a, b), jnp.where(low, b, a)], axis=1).reshape(T, T)
        return c

    def along_x(vs):
        vs = [jnp.concatenate([split(v[:, :H], 1), split(v[:, H:], 1)], axis=0) for v in vs]
        vs = [dot(v, xw[...], NN) for v in vs]
        vs = [v[:, :H] + v[:, H:] for v in vs]
        return [jnp.concatenate([v[:H], v[H:]], axis=1) for v in vs]

    def along_y(vs, ws):
        vs = [split(v, 0) for v in vs]
        vs = [dot(w[...], v, NN) for v, w in zip(vs, ws)]
        return [v[:H] + v[H:] for v in vs]

    def step_mid(i, c):
        js = [i * um + k for k in range(um)]
        at = [(j, kind) for j in js for kind in range(2)]
        rows = [pl.ds(pl.multiple_of(j * 16 + 8 * kind, 8), 8) for j, kind in at]
        ws = [(y0, y1)[kind] for _, kind in at]
        vs = [buf[:, r, :].reshape(H, T) for r in rows]
        vs = along_y(along_x(vs), ws)
        ks = [kt[2 * j + kind] for j, kind in at]
        vs = [v * jnp.concatenate([k, k], axis=1) for v, k in zip(vs, ks)]
        vs = along_x(along_y(vs, ws))
        for r, v in zip(rows, vs):
            buf[:, r, :] = v.reshape(n, 8, T)
        return c

    row = lax.broadcasted_iota(jnp.int32, (T, T), 0)
    col = lax.broadcasted_iota(jnp.int32, (T, T), 1)
    eye = (row == col).astype(jnp.float32).astype(jnp.bfloat16)
    fold = (row[:G] == col[:G] % G).astype(jnp.float32).astype(jnp.bfloat16)

    def step_out(i, c):
        ts = [i * uo + k for k in range(uo)]
        phis = [dot(eye, partners(t).reshape(T, T), NT) for t in ts]
        vs = []
        for t in ts:
            v = buf[t].reshape(n, 2, 8, T)
            vs.append((jnp.where(low, v[:, 0], v[:, 1]), zoa))
            vs.append((jnp.where(low, v[:, 1], v[:, 0]), zob))
        vs = [(split(v.reshape(H, T), 0), w) for v, w in vs]
        vs = [dot(w[...], v, NN) for v, w in vs]
        vs = [v[:H] + v[H:] for v in vs]
        vs = [v * phis[k // 2][H * (k % 2) : H * (k % 2) + H] for k, v in enumerate(vs)]
        vs = [split(v[:, :H] + v[:, H:], 1) for v in vs]
        for k, t in enumerate(ts):
            v = dot(fold, jnp.concatenate(vs[2 * k : 2 * k + 2], axis=0), NT)
            if not first:
                v = acc[:, lanes(t)] + v
                c = jnp.maximum(c, jnp.maximum(jnp.abs(v[:, :H]), jnp.abs(v[:, H:])))
            out[:, lanes(t)] = v
        return c

    lax.fori_loop(0, n // ui, step_in, 0)
    lax.fori_loop(0, n // um, step_mid, 0)
    largest = lax.fori_loop(0, n // uo, step_out, jnp.zeros((G, H), jnp.float32))
    if not first:
        power = jnp.full((G, H), jnp.clip(jnp.max(largest), 1e-30, 1e30), jnp.float32)
        power = jnp.round(jnp.log2(power))
        scale = jnp.tile(jnp.exp2(-power), (1, T // H))
        out[:, G * G :] = power

        def step_code(t, c):
            v = out[:, lanes(t)] * scale
            out[:, lanes(t)] = v * jnp.abs(v) * 4096.0
            return c

        lax.fori_loop(0, n, step_code, 0, unroll=4)


def pair_terms(own, parts, acc, tabs, kt, steps=(8, 8, 8)):
    vm = pl.BlockSpec(memory_space=pltpu.VMEM)
    first = acc is None
    args = (own, *parts, tabs, kt) + (() if first else (acc,))
    return pl.pallas_call(
        functools.partial(pair_kernel, steps, first),
        out_shape=jax.ShapeDtypeStruct((G, G * G + (0 if first else H)), jnp.float32),
        in_specs=[vm] * len(args),
        out_specs=vm,
        scratch_shapes=[pltpu.VMEM((T // 16, T, T), jnp.float32)],
        compiler_params=pltpu.CompilerParams(vmem_limit_bytes=40 * 1024 * 1024),
        cost_estimate=pl.CostEstimate(flops=13 * 16 * 2 * T**3, bytes_accessed=8 << 20, transcendentals=0),
        name="pair_first" if first else "pair_second",
    )(*args)


def pick_kernel(at, orbitals, low, high, both, own, sems):
    half = 2 * at[0]
    copies = [
        pltpu.make_async_copy(orbitals.at[pl.ds(half, 1)], low, sems.at[0]),
        pltpu.make_async_copy(orbitals.at[pl.ds(half + 1, 1)], high, sems.at[1]),
        pltpu.make_async_copy(orbitals.at[pl.ds(half, 2)], both, sems.at[2]),
        pltpu.make_async_copy(orbitals.at[pl.ds(at[1], 1)], own, sems.at[3]),
    ]
    for copy in copies:
        copy.start()
    for copy in copies:
        copy.wait()


def pick(orbitals, half, mine):
    vm = pl.BlockSpec(memory_space=pltpu.VMEM)
    return pl.pallas_call(
        pick_kernel,
        out_shape=[jax.ShapeDtypeStruct((k, *orbitals.shape[1:]), orbitals.dtype) for k in (1, 1, 2, 1)],
        in_specs=[pl.BlockSpec(memory_space=pltpu.SMEM), pl.BlockSpec(memory_space=pltpu.HBM)],
        out_specs=[vm] * 4,
        scratch_shapes=[pltpu.SemaphoreType.DMA((4,))],
        compiler_params=pltpu.CompilerParams(vmem_limit_bytes=8 * 1024 * 1024),
        name="pick",
    )(jnp.stack([half, mine]).astype(jnp.int32), orbitals)


def decoded(slabs, power):
    v = slabs.astype(jnp.float32)
    root = jnp.sqrt(jnp.abs(v)) * power
    return jnp.where(v < 0, -root, root)


def body(orbitals):
    groups, blocks = lax.axis_size("grp"), lax.axis_size("band")
    halves = groups // 2

    def source(g, b, distance):
        s = (b + distance) % blocks
        crosses = b // 4 != s // 4
        return (g ^ 1 if crosses else g) * blocks + s

    def move(v, distances):
        pairs = [(source(g, b, distances[b % 2]), g * blocks + b) for g in range(groups) for b in range(blocks)]
        return lax.ppermute(v, ("grp", "band"), pairs)

    chip, near, far = (1, -1), (-1, 1), (-2, 2)
    group = lax.axis_index("grp")
    low, high, both, own = pick(orbitals, group // halves, group % halves)
    near_low = move(low, near)
    on_chip = move(both, chip)
    near_high = move(high, near)
    kt = kernel_table()
    near_low, kt = lax.optimization_barrier((near_low, kt))
    far_both = move(both, far)
    swapped_low = move(near_low, chip)
    tabs = tables()
    row = pair_terms(own, (on_chip, near_low, swapped_low), None, tabs, kt)
    swapped_high = move(near_high, chip)
    row = pair_terms(own, (far_both, near_high, swapped_high), row, tabs, kt)
    slabs = row.astype(jnp.float16).reshape(groups, G // groups, -1)
    slabs = lax.all_to_all(slabs, "grp", split_axis=0, concat_axis=0, tiled=True)
    slabs, power = slabs[..., : G * G], slabs[:, :1, G * G : G * G + 1]
    power = jnp.exp2(power.astype(jnp.float32)) * (1.0 / 64.0)
    return decoded(slabs[:halves], power[:halves]) + decoded(slabs[halves:], power[halves:])


def solution(mesh):
    return jax.shard_map(
        body,
        mesh=mesh,
        in_specs=(P("band", None, None),),
        out_specs=P("band", "grp", None),
        check_vma=False,
    )
```

```python
import functools
import math

import jax
import jax.numpy as jnp
import ml_dtypes
import numpy as np
from jax import lax
from jax.experimental import pallas as pl
from jax.experimental.pallas import tpu as pltpu
from jax.sharding import PartitionSpec as P

CELL_LENGTH = 41.05
SCREENING = 0.106
G = 64
H = 128
T = 256
CODE_SHIFT = 118
CUTS = 2


def split_table(m):
    hi = m.astype(ml_dtypes.bfloat16)
    lo = (m - hi.astype(np.float64)).astype(ml_dtypes.bfloat16)
    return np.block([[hi, hi], [lo, lo]])


def row_of(kind, r):
    s, kz, y = r % 8 // 4, r // 2 % 2, r % 2
    return 4 * (r // 8) + 2 * (s ^ kind) + y, 2 * kind + kz


def tables():
    i = np.arange(G)
    ang = 2 * np.pi * ((i[:, None] * i[None, :]) % G) / G
    h = (np.cos(ang) + np.sin(ang)) / 8.0
    r = np.arange(H)
    out = []
    for kind in range(2):
        kz = 4 * (r // 8) + 2 * ((r // 4 % 2) ^ kind) + r // 2 % 2
        m = (r[:, None] % 2 == r[None, :] // G) * h[kz[:, None], r[None, :] % G]
        out += [split_table(m), split_table(m.T)]
    for kind in range(2):
        y, kz = row_of(kind, r)
        out.append(split_table((kz[:, None] == kz[None, :]) * h[y[:, None], y[None, :]]))
    out.append(split_table(np.kron(np.eye(2), h)).T)
    return jnp.asarray(np.stack(out))


def kernel_table():
    s = (T // 8, H, H)
    j = lax.broadcasted_iota(jnp.int32, s, 0)
    r = lax.broadcasted_iota(jnp.int32, s, 1)
    l = lax.broadcasted_iota(jnp.int32, s, 2)

    def wave(k):
        return jnp.where(k < G // 2, k, k - G)

    y, kz = row_of(j % 2, r)
    a, b, c = wave(l % G), wave(y), wave(4 * (j // 2) + kz)
    q = (a * a + b * b + c * c).astype(jnp.float32)
    squared = q * (2.0 * math.pi / CELL_LENGTH) ** 2
    safe = jnp.where(squared > 0, squared, 1.0)
    screened = 4.0 * math.pi * (1.0 - jnp.exp(-safe / (4.0 * SCREENING * SCREENING))) / safe
    return -0.25 * jnp.where(squared > 0, screened, math.pi / (SCREENING * SCREENING))


NN = (((1,), (0,)), ((), ()))
NT = (((1,), (1,)), ((), ()))


def dot(a, b, dims):
    return lax.dot_general(a, b, dims, preferred_element_type=jnp.float32)


def split(v, axis):
    hi = v.astype(jnp.bfloat16)
    lo = (v - hi.astype(jnp.float32)).astype(jnp.bfloat16)
    return jnp.concatenate([hi, lo], axis=axis)


def pair_kernel(steps, own_hbm, pa_hbm, pb_hbm, pc_hbm, pd_hbm, tabs_hbm, kt_hbm, out, *scratch):
    ui, um, uo = steps
    own, pa, pb, pc, pd, tabs, kt, buf, row_buf, sems = scratch
    tabs_copy = pltpu.make_async_copy(tabs_hbm, tabs, sems.at[0])
    kt_copy = pltpu.make_async_copy(kt_hbm, kt, sems.at[1])
    size = G * G // CUTS
    band_copies = []
    for c in range(CUTS):
        at = pl.ds(c * size, size)
        for k, (a, b) in enumerate(((own_hbm, own), (pa_hbm, pa), (pb_hbm, pb), (pc_hbm, pc), (pd_hbm, pd))):
            band_copies.append(pltpu.make_async_copy(a.at[:, :, at], b.at[:, :, at], sems.at[2 + 5 * c + k]))
    for copy in (tabs_copy, *band_copies, kt_copy):
        copy.start()
    tabs_copy.wait()
    zia, zoa, zib, zob, y0, y1, xw = (tabs.at[k] for k in range(7))
    n = T // 16
    low = lax.broadcasted_iota(jnp.int32, (n, 8, T), 1) < 4

    def lanes(t, size=T):
        return pl.ds(pl.multiple_of(t * size, size), size)

    def partners(t, size=T):
        return jnp.concatenate([p[:, :, lanes(t, size)] for p in (pa, pb, pc, pd)], axis=0)

    def step_in(i, c):
        ts = [i * ui + k for k in range(ui)]

        def product(u):
            phi = own[:, :, lanes(u, H)].astype(jnp.float32)
            return split((partners(u, H).astype(jnp.float32) * phi).reshape(T, H), 1)

        ds = [(product(2 * t + s), (zia, zib)[s]) for t in ts for s in range(2)]
        vs = [dot(w[...], d, NT) for d, w in ds]
        vs = [(v[:H] + v[H:]).reshape(n, 8, T) for v in vs]
        for k, t in enumerate(ts):
            a, b = vs[2 * k], vs[2 * k + 1]
            buf[t] = jnp.stack([jnp.where(low, a, b), jnp.where(low, b, a)], axis=1).reshape(T, T)
        return c

    def along_x(vs):
        vs = [jnp.concatenate([split(v[:, :H], 1), split(v[:, H:], 1)], axis=0) for v in vs]
        vs = [dot(v, xw[...], NN) for v in vs]
        vs = [v[:, :H] + v[:, H:] for v in vs]
        return [jnp.concatenate([v[:H], v[H:]], axis=1) for v in vs]

    def along_y(vs, ws):
        vs = [split(v, 0) for v in vs]
        vs = [dot(w[...], v, NN) for v, w in zip(vs, ws)]
        return [v[:H] + v[H:] for v in vs]

    def step_mid(i, c):
        js = [i * um + k for k in range(um)]
        at = [(j, kind) for j in js for kind in range(2)]
        rows = [pl.ds(pl.multiple_of(j * 16 + 8 * kind, 8), 8) for j, kind in at]
        ws = [(y0, y1)[kind] for _, kind in at]
        vs = [buf[:, r, :].reshape(H, T) for r in rows]
        vs = along_y(along_x(vs), ws)
        ks = [kt[2 * j + kind] for j, kind in at]
        vs = [v * jnp.concatenate([k, k], axis=1) for v, k in zip(vs, ks)]
        vs = along_x(along_y(vs, ws))
        for r, v in zip(rows, vs):
            buf[:, r, :] = v.reshape(n, 8, T)
        return c

    row = lax.broadcasted_iota(jnp.int32, (T, T), 0)
    col = lax.broadcasted_iota(jnp.int32, (T, T), 1)
    eye = (row == col).astype(jnp.float32).astype(jnp.bfloat16)
    fold = (row[:G] == col[:G] % G).astype(jnp.float32).astype(jnp.bfloat16)

    def step_out(i, c):
        ts = [i * uo + k for k in range(uo)]
        phis = [dot(eye, partners(t).reshape(T, T), NT) for t in ts]
        vs = []
        for t in ts:
            v = buf[t].reshape(n, 2, 8, T)
            vs.append((jnp.where(low, v[:, 0], v[:, 1]), zoa))
            vs.append((jnp.where(low, v[:, 1], v[:, 0]), zob))
        vs = [(split(v.reshape(H, T), 0), w) for v, w in vs]
        vs = [dot(w[...], v, NN) for v, w in vs]
        vs = [v[:H] + v[H:] for v in vs]
        vs = [v * phis[k // 2][H * (k % 2) : H * (k % 2) + H] for k, v in enumerate(vs)]
        vs = [split(v[:, :H] + v[:, H:], 1) for v in vs]
        for k, t in enumerate(ts):
            v = dot(fold, jnp.concatenate(vs[2 * k : 2 * k + 2], axis=0), NT)
            c = jnp.maximum(c, jnp.maximum(jnp.abs(v[:, :H]), jnp.abs(v[:, H:])))
            row_buf[:, lanes(t)] = v
        return c

    for c in range(CUTS):
        for copy in band_copies[5 * c : 5 * c + 5]:
            copy.wait()
        lax.fori_loop(c * n // ui // CUTS, (c + 1) * n // ui // CUTS, step_in, 0)
    kt_copy.wait()
    lax.fori_loop(0, n // um, step_mid, 0)
    largest = lax.fori_loop(0, n // uo, step_out, jnp.zeros((G, H), jnp.float32))
    power = jnp.full((G, H), jnp.clip(jnp.max(largest), 1e-30, 1e30), jnp.float32)
    power = jnp.round(jnp.log2(power))
    scale = jnp.tile(jnp.exp2(-power), (1, T // H))
    out[:, G * G :] = power.astype(out.dtype)

    def step_code(t, c):
        v = row_buf[:, lanes(t)] * scale
        r = v * v
        r = r * r
        r = r * r * 2.0 ** (CODE_SHIFT // 2)
        r = r * r
        out[:, lanes(t)] = jnp.where(v < 0, -r, r).astype(out.dtype)
        return c

    lax.fori_loop(0, n, step_code, 0, unroll=4)


def pair_row(own, parts, tabs, kt, limit_mib, steps=(8, 8, 8)):
    args = (own, *parts, tabs, kt)
    return pl.pallas_call(
        functools.partial(pair_kernel, steps),
        out_shape=jax.ShapeDtypeStruct((G, G * G + H), jnp.bfloat16),
        in_specs=[pl.BlockSpec(memory_space=pl.ANY)] * len(args),
        out_specs=pl.BlockSpec(memory_space=pltpu.VMEM),
        scratch_shapes=[
            *(pltpu.VMEM(v.shape, v.dtype) for v in args),
            pltpu.VMEM((T // 16, T, T), jnp.float32),
            pltpu.VMEM((G, G * G), jnp.float32),
            pltpu.SemaphoreType.DMA((2 + 5 * CUTS,)),
        ],
        compiler_params=pltpu.CompilerParams(vmem_limit_bytes=limit_mib * 1024 * 1024),
        cost_estimate=pl.CostEstimate(flops=13 * 16 * 2 * T**3, bytes_accessed=8 << 20, transcendentals=0),
        name="pair_row",
    )(*args)


def gather_kernel(count, *refs):
    *earlier, slabs, out = refs
    first = 0
    for ref in earlier:
        out[: ref.shape[0]] = ref[...]
        first += ref.shape[0]
    size = slabs.shape[-1] - H
    wide = 4 * H

    def step(t, c):
        at = pl.ds(pl.multiple_of(t * wide, wide), wide)
        for k in range(count):
            total = None
            for s in range(k, slabs.shape[0], count):
                v = slabs[s, :, at].astype(jnp.float32)
                power = slabs[s, :, size:].astype(jnp.float32) - CODE_SHIFT / 16
                v_root = jnp.exp2(jnp.log2(jnp.abs(v)) * (1 / 16) + jnp.tile(power, (1, wide // H)))
                v = jnp.where(v == 0, 0.0, jnp.where(v < 0, -v_root, v_root))
                total = v if total is None else total + v
            out[first + k, :, at] = total
        return c

    lax.fori_loop(0, size // wide, step, 0, unroll=2)


def gathered(slabs, count, earlier=()):
    vm = pl.BlockSpec(memory_space=pltpu.VMEM)
    rows = count + sum(v.shape[0] for v in earlier)
    return pl.pallas_call(
        functools.partial(gather_kernel, count),
        out_shape=jax.ShapeDtypeStruct((rows, slabs.shape[1], slabs.shape[2] - H), jnp.float32),
        in_specs=[vm] * (1 + len(earlier)),
        out_specs=vm,
        compiler_params=pltpu.CompilerParams(vmem_limit_bytes=16 * 1024 * 1024),
        cost_estimate=pl.CostEstimate(flops=1 << 22, bytes_accessed=1 << 20, transcendentals=1 << 19),
        name="gathered",
    )(*earlier, slabs)


def body(orbitals):
    groups, blocks = lax.axis_size("grp"), lax.axis_size("band")
    halves = groups // 4

    def source(g, b, distance):
        s = (b + distance) % blocks
        crosses = b // 4 != s // 4
        return (g ^ 1 if crosses else g) * blocks + s

    def move(v, distances):
        pairs = [(source(g, b, distances[b % 2]), g * blocks + b) for g in range(groups) for b in range(blocks)]
        return lax.ppermute(v, ("grp", "band"), pairs)

    def spread(row):
        slabs = row.reshape(groups, G // groups, -1)
        return lax.all_to_all(slabs, "grp", split_axis=0, concat_axis=0, tiled=True)

    chip, near, far = (1, -1), (-1, 1), (-2, 2)
    group = lax.axis_index("grp")
    mine = lax.dynamic_slice_in_dim(orbitals, group // halves, 1, 0)
    from_near = move(mine, near)
    from_chip = move(mine, chip)
    kt = kernel_table()
    from_far = move(mine, far)
    swapped = move(from_near, chip)
    parts = (from_chip, from_near, swapped, from_far)
    tabs = tables()
    owns = [lax.dynamic_slice_in_dim(orbitals, group % halves + k, 1, 0) for k in range(0, 2 * halves, halves)]
    row = pair_row(owns[0], parts, tabs, kt, 40)
    slabs = spread(row)
    low = gathered(slabs, halves)
    row = pair_row(owns[1], parts, tabs, kt, 62)
    slabs = spread(row)
    return gathered(slabs, halves, (low,))


def solution(mesh):
    return jax.shard_map(
        body,
        mesh=mesh,
        in_specs=(P("band", None, None),),
        out_specs=P("band", "grp", None),
        check_vma=False,
    )
```

```python
import functools
import math

import jax
import jax.numpy as jnp
import ml_dtypes
import numpy as np
from jax import lax
from jax.experimental import pallas as pl
from jax.experimental.pallas import tpu as pltpu
from jax.sharding import PartitionSpec as P

CELL_LENGTH = 41.05
SCREENING = 0.106
G = 64
H = 128
T = 256
CODE_SHIFT = 118


def split_table(m):
    hi = m.astype(ml_dtypes.bfloat16)
    lo = (m - hi.astype(np.float64)).astype(ml_dtypes.bfloat16)
    return np.block([[hi, hi], [lo, lo]])


def row_of(kind, r):
    s, kz, y = r % 8 // 4, r // 2 % 2, r % 2
    return 4 * (r // 8) + 2 * (s ^ kind) + y, 2 * kind + kz


def tables():
    i = np.arange(G)
    ang = 2 * np.pi * ((i[:, None] * i[None, :]) % G) / G
    h = (np.cos(ang) + np.sin(ang)) / 8.0
    r = np.arange(H)
    out = []
    for kind in range(2):
        kz = 4 * (r // 8) + 2 * ((r // 4 % 2) ^ kind) + r // 2 % 2
        m = (r[:, None] % 2 == r[None, :] // G) * h[kz[:, None], r[None, :] % G]
        out += [split_table(m), split_table(m.T)]
    for kind in range(2):
        y, kz = row_of(kind, r)
        out.append(split_table((kz[:, None] == kz[None, :]) * h[y[:, None], y[None, :]]))
    out.append(split_table(np.kron(np.eye(2), h)).T)
    return jnp.asarray(np.stack(out))


def kernel_table():
    s = (T // 8, H, H)
    j = lax.broadcasted_iota(jnp.int32, s, 0)
    r = lax.broadcasted_iota(jnp.int32, s, 1)
    l = lax.broadcasted_iota(jnp.int32, s, 2)

    def wave(k):
        return jnp.where(k < G // 2, k, k - G)

    y, kz = row_of(j % 2, r)
    a, b, c = wave(l % G), wave(y), wave(4 * (j // 2) + kz)
    q = (a * a + b * b + c * c).astype(jnp.float32)
    squared = q * (2.0 * math.pi / CELL_LENGTH) ** 2
    safe = jnp.where(squared > 0, squared, 1.0)
    screened = 4.0 * math.pi * (1.0 - jnp.exp(-safe / (4.0 * SCREENING * SCREENING))) / safe
    return -0.25 * jnp.where(squared > 0, screened, math.pi / (SCREENING * SCREENING))


NN = (((1,), (0,)), ((), ()))
NT = (((1,), (1,)), ((), ()))


def dot(a, b, dims):
    return lax.dot_general(a, b, dims, preferred_element_type=jnp.float32)


def split(v, axis):
    hi = v.astype(jnp.bfloat16)
    lo = (v - hi.astype(jnp.float32)).astype(jnp.bfloat16)
    return jnp.concatenate([hi, lo], axis=axis)


def lanes(t, size=T):
    return pl.ds(pl.multiple_of(t * size, size), size)


def partners(parts, t, size=T):
    return jnp.concatenate([p[:, :, lanes(t, size)] for p in parts], axis=0)


def convolve(step, own, parts, tabs, kt, buf):
    zia, zib, y0, y1, xw = (tabs.at[k] for k in (0, 2, 4, 5, 6))
    n, _, wide = buf.shape
    low = lax.broadcasted_iota(jnp.int32, (n, 8, wide), 1) < 4

    def step_in(i, c):
        ts = [i * step + k for k in range(step)]

        def product(u):
            phi = own[:, :, lanes(u, H)].astype(jnp.float32)
            return split((partners(parts, u, H).astype(jnp.float32) * phi).reshape(wide, H), 1)

        ds = [(product(2 * t + s), (zia, zib)[s]) for t in ts for s in range(2)]
        vs = [dot(w[...], d, NT) for d, w in ds]
        vs = [(v[:H] + v[H:]).reshape(n, 8, wide) for v in vs]
        for k, t in enumerate(ts):
            a, b = vs[2 * k], vs[2 * k + 1]
            buf[t] = jnp.stack([jnp.where(low, a, b), jnp.where(low, b, a)], axis=1).reshape(T, wide)
        return c

    def along_x(vs):
        cuts = range(0, wide, H)
        vs = [jnp.concatenate([split(v[:, k : k + H], 1) for k in cuts], axis=0) for v in vs]
        vs = [dot(v, xw[...], NN) for v in vs]
        vs = [v[:, :H] + v[:, H:] for v in vs]
        return [jnp.concatenate([v[k : k + H] for k in cuts], axis=1) for v in vs]

    def along_y(vs, ws):
        vs = [split(v, 0) for v in vs]
        vs = [dot(w[...], v, NN) for v, w in zip(vs, ws)]
        return [v[:H] + v[H:] for v in vs]

    def step_mid(i, c):
        js = [i * step + k for k in range(step)]
        at = [(j, kind) for j in js for kind in range(2)]
        rows = [pl.ds(pl.multiple_of(j * 16 + 8 * kind, 8), 8) for j, kind in at]
        ws = [(y0, y1)[kind] for _, kind in at]
        vs = [buf[:, r, :].reshape(H, wide) for r in rows]
        vs = along_y(along_x(vs), ws)
        ks = [jnp.concatenate([kt[2 * j + kind]] * (wide // H), axis=1) for j, kind in at]
        vs = along_x(along_y([v * k for v, k in zip(vs, ks)], ws))
        for r, v in zip(rows, vs):
            buf[:, r, :] = v.reshape(n, 8, wide)
        return c

    lax.fori_loop(0, n // step, step_in, 0)
    lax.fori_loop(0, n // step, step_mid, 0)


def reduce_partners(step, parts, tabs, bufs, acc, out):
    zoa, zob = tabs.at[1], tabs.at[3]
    n = T // 16
    wide = sum(b.shape[2] for b in bufs)
    low = lax.broadcasted_iota(jnp.int32, (n, 8, wide), 1) < 4
    row = lax.broadcasted_iota(jnp.int32, (G, T), 0)
    col = lax.broadcasted_iota(jnp.int32, (G, T), 1)
    fold = (row == col % G).astype(jnp.float32).astype(jnp.bfloat16)

    def step_out(i, c):
        ts = [i * step + k for k in range(step)]
        phis = [partners(parts, t).reshape(wide, T).astype(jnp.float32).T for t in ts]
        vs = []
        for t in ts:
            v = jnp.concatenate([b[t] for b in bufs], axis=1).reshape(n, 2, 8, wide)
            vs.append((jnp.where(low, v[:, 0], v[:, 1]), zoa))
            vs.append((jnp.where(low, v[:, 1], v[:, 0]), zob))
        vs = [(split(v.reshape(H, wide), 0), w) for v, w in vs]
        vs = [dot(w[...], v, NN) for v, w in vs]
        vs = [v[:H] + v[H:] for v in vs]
        vs = [v * phis[k // 2][H * (k % 2) : H * (k % 2) + H] for k, v in enumerate(vs)]
        vs = [split(v[:, :H] + v[:, H:], 1) for v in vs]
        for k, t in enumerate(ts):
            v = dot(fold, jnp.concatenate(vs[2 * k : 2 * k + 2], axis=0), NT)
            if acc is not None:
                v = acc[:, lanes(t)] + v
            c = jnp.maximum(c, jnp.maximum(jnp.abs(v[:, :H]), jnp.abs(v[:, H:])))
            out[:, lanes(t)] = v
        return c

    return lax.fori_loop(0, n // step, step_out, jnp.zeros((G, H), jnp.float32))


def convolve_kernel(step, *refs):
    own, *parts, tabs, kt, out = refs
    convolve(step, own, parts, tabs, kt, out)


def reduce_kernel(step, pa, pb, pc, tabs, buf, out):
    reduce_partners(step, (pa, pb, pc), tabs, (buf,), None, out)


def last_kernel(step, own, pa, pb, pc, tabs, kt, earlier, acc, out, buf, row_buf):
    convolve(step, own, (pc,), tabs, kt, buf)
    largest = reduce_partners(step, (pa, pb, pc), tabs, (earlier, buf), acc, row_buf)
    power = jnp.full((G, H), jnp.clip(jnp.max(largest), 1e-37, 1e37), jnp.float32)
    power = jnp.round(jnp.log2(power))
    scale = jnp.tile(jnp.exp2(-power), (1, T // H))
    out[:, G * G :] = power.astype(out.dtype)

    def step_code(t, c):
        v = row_buf[:, lanes(t)] * scale
        r = v * v
        r = r * r
        r = r * r * 2.0 ** (CODE_SHIFT // 2)
        r = r * r
        out[:, lanes(t)] = jnp.where(v < 0, -r, r).astype(out.dtype)
        return c

    lax.fori_loop(0, T // 16, step_code, 0, unroll=4)


def pair_call(kernel, args, shape, dtype, scratch, work, step=8):
    vm = pl.BlockSpec(memory_space=pltpu.VMEM)
    return pl.pallas_call(
        functools.partial(kernel, step),
        out_shape=jax.ShapeDtypeStruct(shape, dtype),
        in_specs=[vm] * len(args),
        out_specs=vm,
        scratch_shapes=[pltpu.VMEM(s, jnp.float32) for s in scratch],
        compiler_params=pltpu.CompilerParams(vmem_limit_bytes=32 * 1024 * 1024),
        cost_estimate=pl.CostEstimate(flops=work * 16 * 2 * T**3, bytes_accessed=8 << 20, transcendentals=0),
    )(*args)


def pick_kernel(at, orbitals, *refs):
    *outs, sems = refs
    copies = [
        pltpu.make_async_copy(orbitals.at[pl.ds(at[k], out.shape[0])], out, sems.at[k]) for k, out in enumerate(outs)
    ]
    for copy in copies:
        copy.start()
    for copy in copies:
        copy.wait()


def pick(orbitals, starts, counts, limit_mib):
    vm = pl.BlockSpec(memory_space=pltpu.VMEM)
    return pl.pallas_call(
        pick_kernel,
        out_shape=[jax.ShapeDtypeStruct((k, *orbitals.shape[1:]), orbitals.dtype) for k in counts],
        in_specs=[pl.BlockSpec(memory_space=pltpu.SMEM), pl.BlockSpec(memory_space=pltpu.HBM)],
        out_specs=[vm] * len(counts),
        scratch_shapes=[pltpu.SemaphoreType.DMA((len(counts),))],
        compiler_params=pltpu.CompilerParams(vmem_limit_bytes=limit_mib * 1024 * 1024),
        name="pick",
    )(jnp.stack(starts).astype(jnp.int32), pltpu.with_memory_space_constraint(orbitals, pltpu.HBM))


def gather_kernel(slabs, out):
    count, _, size = out.shape
    wide = 4 * H

    def step(t, c):
        at = pl.ds(pl.multiple_of(t * wide, wide), wide)
        for k in range(count):
            total = None
            for s in range(k, slabs.shape[0], count):
                v = slabs[s, :, at].astype(jnp.float32)
                power = slabs[s, :, size:].astype(jnp.float32) - CODE_SHIFT / 16
                root = jnp.exp2(jnp.log2(jnp.abs(v)) * (1 / 16) + jnp.tile(power, (1, wide // H)))
                v = jnp.where(v == 0, 0.0, jnp.where(v < 0, -root, root))
                total = v if total is None else total + v
            out[k, :, at] = total
        return c

    lax.fori_loop(0, size // wide, step, 0, unroll=2)


def gathered(slabs, count):
    vm = pl.BlockSpec(memory_space=pltpu.VMEM)
    return pl.pallas_call(
        gather_kernel,
        out_shape=jax.ShapeDtypeStruct((count, slabs.shape[1], slabs.shape[2] - H), jnp.float32),
        in_specs=[vm],
        out_specs=vm,
        compiler_params=pltpu.CompilerParams(vmem_limit_bytes=16 * 1024 * 1024),
        name="gathered",
    )(slabs)


def body(orbitals):
    groups, blocks = lax.axis_size("grp"), lax.axis_size("band")
    halves = groups // 2

    def source(g, b, distance):
        s = (b + distance) % blocks
        crosses = b // 4 != s // 4
        return (g ^ 1 if crosses else g) * blocks + s

    def move(v, distances):
        pairs = [(source(g, b, distances[b % 2]), g * blocks + b) for g in range(groups) for b in range(blocks)]
        return lax.ppermute(v, ("grp", "band"), pairs)

    chip, near, far = (1, -1), (-1, 1), (-2, 2)
    group = lax.axis_index("grp")
    half = group // halves * 2
    (low,) = pick(orbitals, (half,), (1,), 8)
    near_low = move(low, near)
    high, both, own = pick(orbitals, (half + 1, half, group % halves), (1, 2, 1), 8)
    on_chip = move(both, chip)
    near_high = move(high, near)
    kt = kernel_table()
    near_low, kt = lax.optimization_barrier((near_low, kt))
    far_both = move(both, far)
    swapped_low = move(near_low, chip)
    tabs = tables()
    parts = (on_chip, near_low, swapped_low)
    buf = pair_call(convolve_kernel, (own, *parts, tabs, kt), (T // 16, T, T), jnp.float32, [], 9)
    swapped_high = move(near_high, chip)
    row = pair_call(reduce_kernel, (*parts, tabs, buf), (G, G * G), jnp.float32, [], 3)
    half_buf = (T // 16, T, H)
    near_high, row = lax.optimization_barrier((near_high, row))
    args = (own, near_high, swapped_high, tabs, kt)
    earlier = pair_call(convolve_kernel, args, half_buf, jnp.float32, [], 5)
    args = (own, near_high, swapped_high, far_both, tabs, kt, earlier, row)
    shape = (G, G * G + H)
    row = pair_call(last_kernel, args, shape, jnp.bfloat16, [half_buf, (G, G * G)], 7)
    slabs = row.reshape(groups, G // groups, -1)
    slabs = lax.all_to_all(slabs, "grp", split_axis=0, concat_axis=0, tiled=True)
    return gathered(slabs, halves)


def solution(mesh):
    return jax.shard_map(
        body,
        mesh=mesh,
        in_specs=(P("band", None, None),),
        out_specs=P("band", "grp", None),
        check_vma=False,
    )
```

```python
import functools
import math

import jax
import jax.numpy as jnp
import ml_dtypes
import numpy as np
from jax import lax
from jax.experimental import pallas as pl
from jax.experimental.pallas import tpu as pltpu
from jax.sharding import PartitionSpec as P

CELL_LENGTH = 41.05
SCREENING = 0.106
G = 64
H = 128
T = 256
CODE_SHIFT = 118


def split_table(m):
    hi = m.astype(ml_dtypes.bfloat16)
    lo = (m - hi.astype(np.float64)).astype(ml_dtypes.bfloat16)
    return np.block([[hi, hi], [lo, lo]])


def row_of(kind, r):
    s, kz, y = r % 8 // 4, r // 2 % 2, r % 2
    return 4 * (r // 8) + 2 * (s ^ kind) + y, 2 * kind + kz


def tables():
    i = np.arange(G)
    ang = 2 * np.pi * ((i[:, None] * i[None, :]) % G) / G
    h = (np.cos(ang) + np.sin(ang)) / 8.0
    r = np.arange(H)
    out = []
    for kind in range(2):
        kz = 4 * (r // 8) + 2 * ((r // 4 % 2) ^ kind) + r // 2 % 2
        m = (r[:, None] % 2 == r[None, :] // G) * h[kz[:, None], r[None, :] % G]
        out += [split_table(m), split_table(m.T)]
    for kind in range(2):
        y, kz = row_of(kind, r)
        out.append(split_table((kz[:, None] == kz[None, :]) * h[y[:, None], y[None, :]]))
    out.append(split_table(np.kron(np.eye(2), h)).T)
    return jnp.asarray(np.stack(out))


def kernel_table():
    s = (T // 8, H, H)
    j = lax.broadcasted_iota(jnp.int32, s, 0)
    r = lax.broadcasted_iota(jnp.int32, s, 1)
    l = lax.broadcasted_iota(jnp.int32, s, 2)

    def wave(k):
        return jnp.where(k < G // 2, k, k - G)

    y, kz = row_of(j % 2, r)
    a, b, c = wave(l % G), wave(y), wave(4 * (j // 2) + kz)
    q = (a * a + b * b + c * c).astype(jnp.float32)
    squared = q * (2.0 * math.pi / CELL_LENGTH) ** 2
    safe = jnp.where(squared > 0, squared, 1.0)
    screened = 4.0 * math.pi * (1.0 - jnp.exp(-safe / (4.0 * SCREENING * SCREENING))) / safe
    return -0.25 * jnp.where(squared > 0, screened, math.pi / (SCREENING * SCREENING))


NN = (((1,), (0,)), ((), ()))
NT = (((1,), (1,)), ((), ()))


def dot(a, b, dims):
    return lax.dot_general(a, b, dims, preferred_element_type=jnp.float32)


def split(v, axis):
    hi = v.astype(jnp.bfloat16)
    lo = (v - hi.astype(jnp.float32)).astype(jnp.bfloat16)
    return jnp.concatenate([hi, lo], axis=axis)


def pair_kernel(steps, first, *refs):
    ui, um, uo = steps
    own, pa, pb, pc, tabs, kt = refs[:6]
    acc = None if first else refs[6]
    out, buf, row_buf = refs[-3:]
    if first:
        row_buf = out
    zia, zoa, zib, zob, y0, y1, xw = (tabs.at[k] for k in range(7))
    n = T // 16
    low = lax.broadcasted_iota(jnp.int32, (n, 8, T), 1) < 4

    def lanes(t, size=T):
        return pl.ds(pl.multiple_of(t * size, size), size)

    def partners(t, size=T):
        return jnp.concatenate([p[:, :, lanes(t, size)] for p in (pa, pb, pc)], axis=0)

    def step_in(i, c):
        ts = [i * ui + k for k in range(ui)]

        def product(u):
            phi = own[:, :, lanes(u, H)].astype(jnp.float32)
            return split((partners(u, H).astype(jnp.float32) * phi).reshape(T, H), 1)

        ds = [(product(2 * t + s), (zia, zib)[s]) for t in ts for s in range(2)]
        vs = [dot(w[...], d, NT) for d, w in ds]
        vs = [(v[:H] + v[H:]).reshape(n, 8, T) for v in vs]
        for k, t in enumerate(ts):
            a, b = vs[2 * k], vs[2 * k + 1]
            buf[t] = jnp.stack([jnp.where(low, a, b), jnp.where(low, b, a)], axis=1).reshape(T, T)
        return c

    def along_x(vs):
        vs = [jnp.concatenate([split(v[:, :H], 1), split(v[:, H:], 1)], axis=0) for v in vs]
        vs = [dot(v, xw[...], NN) for v in vs]
        vs = [v[:, :H] + v[:, H:] for v in vs]
        return [jnp.concatenate([v[:H], v[H:]], axis=1) for v in vs]

    def along_y(vs, ws):
        vs = [split(v, 0) for v in vs]
        vs = [dot(w[...], v, NN) for v, w in zip(vs, ws)]
        return [v[:H] + v[H:] for v in vs]

    def step_mid(i, c):
        js = [i * um + k for k in range(um)]
        at = [(j, kind) for j in js for kind in range(2)]
        rows = [pl.ds(pl.multiple_of(j * 16 + 8 * kind, 8), 8) for j, kind in at]
        ws = [(y0, y1)[kind] for _, kind in at]
        vs = [buf[:, r, :].reshape(H, T) for r in rows]
        vs = along_y(along_x(vs), ws)
        ks = [kt[2 * j + kind] for j, kind in at]
        vs = [v * jnp.concatenate([k, k], axis=1) for v, k in zip(vs, ks)]
        vs = along_x(along_y(vs, ws))
        for r, v in zip(rows, vs):
            buf[:, r, :] = v.reshape(n, 8, T)
        return c

    row = lax.broadcasted_iota(jnp.int32, (T, T), 0)
    col = lax.broadcasted_iota(jnp.int32, (T, T), 1)
    fold = (row[:G] == col[:G] % G).astype(jnp.float32).astype(jnp.bfloat16)

    def step_out(i, c):
        ts = [i * uo + k for k in range(uo)]
        phis = [partners(t).reshape(T, T).astype(jnp.float32).T for t in ts]
        vs = []
        for t in ts:
            v = buf[t].reshape(n, 2, 8, T)
            vs.append((jnp.where(low, v[:, 0], v[:, 1]), zoa))
            vs.append((jnp.where(low, v[:, 1], v[:, 0]), zob))
        vs = [(split(v.reshape(H, T), 0), w) for v, w in vs]
        vs = [dot(w[...], v, NN) for v, w in vs]
        vs = [v[:H] + v[H:] for v in vs]
        vs = [v * phis[k // 2][H * (k % 2) : H * (k % 2) + H] for k, v in enumerate(vs)]
        vs = [split(v[:, :H] + v[:, H:], 1) for v in vs]
        for k, t in enumerate(ts):
            v = dot(fold, jnp.concatenate(vs[2 * k : 2 * k + 2], axis=0), NT)
            if not first:
                v = acc[:, lanes(t)] + v
                c = jnp.maximum(c, jnp.maximum(jnp.abs(v[:, :H]), jnp.abs(v[:, H:])))
            row_buf[:, lanes(t)] = v
        return c

    lax.fori_loop(0, n // ui, step_in, 0)
    lax.fori_loop(0, n // um, step_mid, 0)
    largest = lax.fori_loop(0, n // uo, step_out, jnp.zeros((G, H), jnp.float32))
    if not first:
        power = jnp.full((G, H), jnp.clip(jnp.max(largest), 1e-37, 1e37), jnp.float32)
        power = jnp.round(jnp.log2(power))
        scale = jnp.tile(jnp.exp2(-power), (1, T // H))
        out[:, G * G :] = power.astype(out.dtype)

        def step_code(t, c):
            v = row_buf[:, lanes(t)] * scale
            r = v * v
            r = r * r
            r = r * r * 2.0 ** (CODE_SHIFT // 2)
            r = r * r
            out[:, lanes(t)] = jnp.where(v < 0, -r, r).astype(out.dtype)
            return c

        lax.fori_loop(0, n, step_code, 0, unroll=4)


def pair_terms(own, parts, acc, tabs, kt, steps=(16, 8, 16)):
    vm = pl.BlockSpec(memory_space=pltpu.VMEM)
    first = acc is None
    args = (own, *parts, tabs, kt) + (() if first else (acc,))
    return pl.pallas_call(
        functools.partial(pair_kernel, steps, first),
        out_shape=jax.ShapeDtypeStruct((G, G * G), jnp.float32) if first else jax.ShapeDtypeStruct((G, G * G + H), jnp.bfloat16),
        in_specs=[vm] * len(args),
        out_specs=vm,
        scratch_shapes=[pltpu.VMEM((T // 16, T, T), jnp.float32), pltpu.VMEM((G, G * G), jnp.float32)],
        compiler_params=pltpu.CompilerParams(vmem_limit_bytes=40 * 1024 * 1024),
        cost_estimate=pl.CostEstimate(flops=13 * 16 * 2 * T**3, bytes_accessed=8 << 20, transcendentals=0),
        name="pair_first" if first else "pair_second",
    )(*args)


def pick_kernel(at, orbitals, *refs):
    *outs, sems = refs
    copies = [
        pltpu.make_async_copy(orbitals.at[pl.ds(at[k], out.shape[0])], out, sems.at[k]) for k, out in enumerate(outs)
    ]
    for copy in copies:
        copy.start()
    for copy in copies:
        copy.wait()


def pick(orbitals, starts, counts, limit_mib):
    vm = pl.BlockSpec(memory_space=pltpu.VMEM)
    return pl.pallas_call(
        pick_kernel,
        out_shape=[jax.ShapeDtypeStruct((k, *orbitals.shape[1:]), orbitals.dtype) for k in counts],
        in_specs=[pl.BlockSpec(memory_space=pltpu.SMEM), pl.BlockSpec(memory_space=pltpu.HBM)],
        out_specs=[vm] * len(counts),
        scratch_shapes=[pltpu.SemaphoreType.DMA((len(counts),))],
        compiler_params=pltpu.CompilerParams(vmem_limit_bytes=limit_mib * 1024 * 1024),
        name="pick",
    )(jnp.stack(starts).astype(jnp.int32), pltpu.with_memory_space_constraint(orbitals, pltpu.HBM))


def gather_kernel(slabs, out):
    count, _, size = out.shape
    wide = 4 * H

    def step(t, c):
        at = pl.ds(pl.multiple_of(t * wide, wide), wide)
        for k in range(count):
            total = None
            for s in range(k, slabs.shape[0], count):
                v = slabs[s, :, at].astype(jnp.float32)
                power = slabs[s, :, size:].astype(jnp.float32) - CODE_SHIFT / 16
                root = jnp.exp2(jnp.log2(jnp.abs(v)) * (1 / 16) + jnp.tile(power, (1, wide // H)))
                v = jnp.where(v == 0, 0.0, jnp.where(v < 0, -root, root))
                total = v if total is None else total + v
            out[k, :, at] = total
        return c

    lax.fori_loop(0, size // wide, step, 0, unroll=8)


def gathered(slabs, count):
    vm = pl.BlockSpec(memory_space=pltpu.VMEM)
    return pl.pallas_call(
        gather_kernel,
        out_shape=jax.ShapeDtypeStruct((count, slabs.shape[1], slabs.shape[2] - H), jnp.float32),
        in_specs=[vm],
        out_specs=vm,
        compiler_params=pltpu.CompilerParams(vmem_limit_bytes=16 * 1024 * 1024),
        name="gathered",
    )(slabs)


def body(orbitals):
    groups, blocks = lax.axis_size("grp"), lax.axis_size("band")
    halves = groups // 2

    def source(g, b, distance):
        s = (b + distance) % blocks
        crosses = b // 4 != s // 4
        return (g ^ 1 if crosses else g) * blocks + s

    def move(v, distances):
        pairs = [(source(g, b, distances[b % 2]), g * blocks + b) for g in range(groups) for b in range(blocks)]
        return lax.ppermute(v, ("grp", "band"), pairs)

    chip, near, far = (1, -1), (-1, 1), (-2, 2)
    group = lax.axis_index("grp")
    half = group // halves * 2
    (low,) = pick(orbitals, (half,), (1,), 8)
    near_low = move(low, near)
    high, both, own = pick(orbitals, (half + 1, half, group % halves), (1, 2, 1), 8)
    on_chip = move(both, chip)
    near_high = move(high, near)
    kt = kernel_table()
    near_low, kt = lax.optimization_barrier((near_low, kt))
    far_both = move(both, far)
    swapped_low = move(near_low, chip)
    tabs = tables()
    row = pair_terms(own, (on_chip, near_low, swapped_low), None, tabs, kt)
    swapped_high = move(near_high, chip)
    row = pair_terms(own, (far_both, near_high, swapped_high), row, tabs, kt)
    slabs = row.reshape(groups, G // groups, -1)
    slabs = lax.all_to_all(slabs, "grp", split_axis=0, concat_axis=0, tiled=True)
    return gathered(slabs, halves)


def solution(mesh):
    return jax.shard_map(
        body,
        mesh=mesh,
        in_specs=(P("band", None, None),),
        out_specs=P("band", "grp", None),
        check_vma=False,
    )
```
